32 devices in a mesh: rep: 4 (over z), fsdp: 2 (over x), seq: 4 (over y, core).
Axes of the slice: x: 2, y: 2, z: 4, core: 2. Of those that a mesh axis runs over, the one named last changes fastest.
Arguments:
- tokens: bfloat16 [8, 1024, 1024], P(('rep', 'fsdp'), 'seq'), may hold values from -6 to 6
- segment_ids: int32 [8, 1024], P(('rep', 'fsdp'), 'seq'), may hold values from 0 to 2, never falling along the last dimension, each value on 1 to 512 neighbouring positions
- cotangent: bfloat16 [8, 1024, 1024], P(('rep', 'fsdp'), 'seq'), may hold values from -6 to 6
- norm_gains: float32 [2, 1024], P(None, 'fsdp'), may hold values from 0.5 to 1.5
- query_key: float32 [2, 1024, 256], P(None, 'fsdp'), may hold values from -0.1875 to 0.1875
- value_gate: float32 [2, 1024, 512], P(None, 'fsdp'), may hold values from -0.1875 to 0.1875
- decay_down: float32 [1024, 16], P('fsdp'), may hold values from -0.1875 to 0.1875
- decay_up: float32 [16, 256], P(None, 'fsdp'), may hold values from -1.5 to 1.5
- decay_bias: float32 [256], P('fsdp'), may hold values from 0.5 to 5
- group_gain: float32 [256], P('fsdp'), may hold values from 0.5 to 1.5
- out_weight: float32 [512, 1024], P('fsdp'), may hold values from -0.25 to 0.25
- gate_up: float32 [2, 1024, 1408], P(None, 'fsdp'), may hold values from -0.1875 to 0.1875
- down_weight: float32 [1408, 1024], P('fsdp'), may hold values from -0.15625 to 0.15625
- norm_gains_mean: float32 [2, 1024], P(None, 'fsdp'), may hold values from -28 to 28
- query_key_mean: float32 [2, 1024, 256], P(None, 'fsdp'), may hold values from -28 to 28
- value_gate_mean: float32 [2, 1024, 512], P(None, 'fsdp'), may hold values from -28 to 28
- decay_down_mean: float32 [1024, 16], P('fsdp'), may hold values from -28 to 28
- decay_up_mean: float32 [16, 256], P(None, 'fsdp'), may hold values from -28 to 28
- decay_bias_mean: float32 [256], P('fsdp'), may hold values from -28 to 28
- group_gain_mean: float32 [256], P('fsdp'), may hold values from -28 to 28
- out_weight_mean: float32 [512, 1024], P('fsdp'), may hold values from -28 to 28
- gate_up_mean: float32 [2, 1024, 1408], P(None, 'fsdp'), may hold values from -28 to 28
- down_weight_mean: float32 [1408, 1024], P('fsdp'), may hold values from -28 to 28
- norm_gains_square: float32 [2, 1024], P(None, 'fsdp'), may hold values from 16.384 to 409.6
- query_key_square: float32 [2, 1024, 256], P(None, 'fsdp'), may hold values from 16.384 to 409.6
- value_gate_square: float32 [2, 1024, 512], P(None, 'fsdp'), may hold values from 16.384 to 409.6
- decay_down_square: float32 [1024, 16], P('fsdp'), may hold values from 16.384 to 409.6
- decay_up_square: float32 [16, 256], P(None, 'fsdp'), may hold values from 16.384 to 409.6
- decay_bias_square: float32 [256], P('fsdp'), may hold values from 16.384 to 409.6
- group_gain_square: float32 [256], P('fsdp'), may hold values from 16.384 to 409.6
- out_weight_square: float32 [512, 1024], P('fsdp'), may hold values from 16.384 to 409.6
- gate_up_square: float32 [2, 1024, 1408], P(None, 'fsdp'), may hold values from 16.384 to 409.6
- down_weight_square: float32 [1408, 1024], P('fsdp'), may hold values from 16.384 to 409.6
Outputs:
- output: bfloat16 [8, 1024, 1024], P(('rep', 'fsdp'), 'seq')
- grad_tokens: bfloat16 [8, 1024, 1024], P(('rep', 'fsdp'), 'seq')
- norm_gains_grad: float32 [2, 1024], P(None, 'fsdp')
- query_key_grad: float32 [2, 1024, 256], P(None, 'fsdp')
- value_gate_grad: float32 [2, 1024, 512], P(None, 'fsdp')
- decay_down_grad: float32 [1024, 16], P('fsdp')
- decay_up_grad: float32 [16, 256], P(None, 'fsdp')
- decay_bias_grad: float32 [256], P('fsdp')
- group_gain_grad: float32 [256], P('fsdp')
- out_weight_grad: float32 [512, 1024], P('fsdp')
- gate_up_grad: float32 [2, 1024, 1408], P(None, 'fsdp')
- down_weight_grad: float32 [1408, 1024], P('fsdp')
- norm_gains_new: float32 [2, 1024], P(None, 'fsdp')
- query_key_new: float32 [2, 1024, 256], P(None, 'fsdp')
- value_gate_new: float32 [2, 1024, 512], P(None, 'fsdp')
- decay_down_new: float32 [1024, 16], P('fsdp')
- decay_up_new: float32 [16, 256], P(None, 'fsdp')
- decay_bias_new: float32 [256], P('fsdp')
- group_gain_new: float32 [256], P('fsdp')
- out_weight_new: float32 [512, 1024], P('fsdp')
- gate_up_new: float32 [2, 1024, 1408], P(None, 'fsdp')
- down_weight_new: float32 [1408, 1024], P('fsdp')
- norm_gains_mean_new: float32 [2, 1024], P(None, 'fsdp')
- query_key_mean_new: float32 [2, 1024, 256], P(None, 'fsdp')
- value_gate_mean_new: float32 [2, 1024, 512], P(None, 'fsdp')
- decay_down_mean_new: float32 [1024, 16], P('fsdp')
- decay_up_mean_new: float32 [16, 256], P(None, 'fsdp')
- decay_bias_mean_new: float32 [256], P('fsdp')
- group_gain_mean_new: float32 [256], P('fsdp')
- out_weight_mean_new: float32 [512, 1024], P('fsdp')
- gate_up_mean_new: float32 [2, 1024, 1408], P(None, 'fsdp')
- down_weight_mean_new: float32 [1408, 1024], P('fsdp')
- norm_gains_square_new: float32 [2, 1024], P(None, 'fsdp')
- query_key_square_new: float32 [2, 1024, 256], P(None, 'fsdp')
- value_gate_square_new: float32 [2, 1024, 512], P(None, 'fsdp')
- decay_down_square_new: float32 [1024, 16], P('fsdp')
- decay_up_square_new: float32 [16, 256], P(None, 'fsdp')
- decay_bias_square_new: float32 [256], P('fsdp')
- group_gain_square_new: float32 [256], P('fsdp')
- out_weight_square_new: float32 [512, 1024], P('fsdp')
- gate_up_square_new: float32 [2, 1024, 1408], P(None, 'fsdp')
- down_weight_square_new: float32 [1408, 1024], P('fsdp')
The draws below stay inside these ranges and needn't reach their ends.
Inputs may be any that keep to these rules, and one draw needn't show every extreme that they name: `segment_ids`: along each sequence the ids never fall; every id occurs, each on 1 to 512 positions, and one id on exactly 512 positions.
All inputs are finite; a program needn't handle non-finite values.
Results may differ from the reference program's by a relative error of at most 0.03.
Values may be sent and summed in bfloat16 or wider, within the bound.
No kernel may reach another device: no remote copies, remote signals or barrier semaphores. Data moves between devices by JAX's collectives and lax.ppermute only.
A program may use at most 256 MiB of HBM per device.

```python
import math
import jax
import jax.numpy as jnp
import numpy as np
from jax import lax

D = 1024
HEADS = 2
KH = 128
VH = 256
HK = 256
HV = 512
FF = 1408
RANK = 16
BLOCK = 64
LEN = 1024
SEQS = 8
DOCS = 3
DOC_MOST = 512
ADAM_STEP = 3


def shard_levels(rng, extent, split, smallest, top_value):
    level = 1.0
    for position, shards_of in split:
        heights = jax.random.uniform(jax.random.fold_in(jax.random.fold_in(rng, 6), position), (shards_of,), jnp.float32, smallest / len(split), top_value / len(split))
        level = level * jnp.repeat(jnp.exp(heights), extent[position] // shards_of).reshape((-1,) + (1,) * (len(extent) - 1 - position))
    return level


def split_up(amount, total, most, skew):
    weights = [(1 << 20) // math.isqrt(standing ** skew) + 1 for standing in range(2, amount + 1)]
    rest, given = total - most - (amount - 1), [1] * (amount - 1)
    while rest > 0:
        movable = [i for i in range(amount - 1) if given[i] < most]
        pool, budget = sum([weights[i] for i in movable]), rest
        for i in movable:
            extra = min(most - given[i], max(1, budget * weights[i] // pool), rest)
            given[i] = given[i] + extra
            rest = rest - extra
    return np.array([most] + given)


def ragged_sizes(rng, amount, total, limit, skew):
    if amount == 2:
        one = jax.random.randint(rng, (), max(1, total - limit), min(limit, total - 1) + 1)
        return jnp.stack([one, total - one])
    lengths = jnp.asarray(split_up(amount, total, limit, skew), jnp.int32)
    couples = (amount - 1) // 2
    source_of, sink = lengths[1:1 + 2 * couples:2], lengths[2:2 + 2 * couples:2]
    margin = jnp.minimum(source_of - 1, limit - sink)
    shifted = jax.random.randint(jax.random.fold_in(rng, 1), (couples,), 0, 1 << 20) % (margin + 1)
    lengths = lengths.at[1:1 + 2 * couples:2].set(source_of - shifted).at[2:2 + 2 * couples:2].set(sink + shifted)
    return lengths[jax.random.permutation(jax.random.fold_in(rng, 2), amount)]


def scatter_about(rng, shape, deviation, reach, pieces=(), held_as=jnp.bfloat16):
    array = deviation * jax.random.normal(rng, shape, jnp.float32)
    if pieces:
        array = array * shard_levels(rng, shape, pieces, -0.22, 0.18)
    return jnp.clip(array, -reach, reach).astype(held_as)


def setup_inputs(seed: int = 0) -> dict:
    key_list = jax.random.split(jax.random.key(seed), 34)
    return {
        "tokens": scatter_about(key_list[0], (SEQS, LEN, D), 1.0, 6.0, ((0, 8), (1, 4))),
        "segment_ids": jax.vmap(lambda own: jnp.searchsorted(jnp.cumsum(ragged_sizes(own, DOCS, LEN, DOC_MOST, 0)), jnp.arange(LEN), side="right"))(jax.random.split(key_list[1], SEQS)).reshape((SEQS, LEN)).astype(jnp.int32),
        "cotangent": scatter_about(key_list[2], (SEQS, LEN, D), 1.0, 6.0, ((0, 8), (1, 4))),
        "norm_gains": jnp.clip(1.0 + 0.1 * jax.random.normal(key_list[3], (2, D), jnp.float32), 0.5, 1.5),
        "query_key": scatter_about(key_list[4], (2, D, HK), D ** -0.5, 0.1875, ((1, 2),), jnp.float32),
        "value_gate": scatter_about(key_list[5], (2, D, HV), D ** -0.5, 0.1875, ((1, 2),), jnp.float32),
        "decay_down": scatter_about(key_list[6], (D, RANK), D ** -0.5, 0.1875, ((0, 2),), jnp.float32),
        "decay_up": scatter_about(key_list[7], (RANK, HK), RANK ** -0.5, 1.5, ((1, 2),), jnp.float32),
        "decay_bias": jnp.clip(0.5 + 4.5 * jax.random.uniform(key_list[8], (HK,), jnp.float32) ** shard_levels(key_list[8], (HK,), ((0, 2),), -0.2, 0.2), 0.5, 5.0),
        "group_gain": jnp.clip(1.0 + 0.1 * jax.random.normal(key_list[9], (VH,), jnp.float32), 0.5, 1.5),
        "out_weight": scatter_about(key_list[10], (HV, D), HV ** -0.5, 0.25, ((0, 2),), jnp.float32),
        "gate_up": scatter_about(key_list[11], (2, D, FF), D ** -0.5, 0.1875, ((1, 2),), jnp.float32),
        "down_weight": scatter_about(key_list[12], (FF, D), FF ** -0.5, 0.15625, ((0, 2),), jnp.float32),
        "norm_gains_mean": scatter_about(key_list[13], (2, D), (0.05 * (SEQS * LEN) ** 0.5), 28.0, ((1, 2),), jnp.float32),
        "query_key_mean": scatter_about(key_list[14], (2, D, HK), (0.05 * (SEQS * LEN) ** 0.5), 28.0, ((1, 2),), jnp.float32),
        "value_gate_mean": scatter_about(key_list[15], (2, D, HV), (0.05 * (SEQS * LEN) ** 0.5), 28.0, ((1, 2),), jnp.float32),
        "decay_down_mean": scatter_about(key_list[16], (D, RANK), (0.05 * (SEQS * LEN) ** 0.5), 28.0, ((0, 2),), jnp.float32),
        "decay_up_mean": scatter_about(key_list[17], (RANK, HK), (0.05 * (SEQS * LEN) ** 0.5), 28.0, ((1, 2),), jnp.float32),
        "decay_bias_mean": scatter_about(key_list[18], (HK,), (0.05 * (SEQS * LEN) ** 0.5), 28.0, ((0, 2),), jnp.float32),
        "group_gain_mean": scatter_about(key_list[19], (VH,), (0.05 * (SEQS * LEN) ** 0.5), 28.0, ((0, 2),), jnp.float32),
        "out_weight_mean": scatter_about(key_list[20], (HV, D), (0.05 * (SEQS * LEN) ** 0.5), 28.0, ((0, 2),), jnp.float32),
        "gate_up_mean": scatter_about(key_list[21], (2, D, FF), (0.05 * (SEQS * LEN) ** 0.5), 28.0, ((1, 2),), jnp.float32),
        "down_weight_mean": scatter_about(key_list[22], (FF, D), (0.05 * (SEQS * LEN) ** 0.5), 28.0, ((0, 2),), jnp.float32),
        "norm_gains_square": jnp.clip(jnp.exp(math.log(409.6) - 3.218876 * jax.random.uniform(key_list[23], (2, D), jnp.float32) ** shard_levels(key_list[23], (2, D), ((1, 2),), -0.2, 0.2)), 16.384, 409.6),
        "query_key_square": jnp.clip(jnp.exp(math.log(409.6) - 3.218876 * jax.random.uniform(key_list[24], (2, D, HK), jnp.float32) ** shard_levels(key_list[24], (2, D, HK), ((1, 2),), -0.2, 0.2)), 16.384, 409.6),
        "value_gate_square": jnp.clip(jnp.exp(math.log(409.6) - 3.218876 * jax.random.uniform(key_list[25], (2, D, HV), jnp.float32) ** shard_levels(key_list[25], (2, D, HV), ((1, 2),), -0.2, 0.2)), 16.384, 409.6),
        "decay_down_square": jnp.clip(jnp.exp(math.log(409.6) - 3.218876 * jax.random.uniform(key_list[26], (D, RANK), jnp.float32) ** shard_levels(key_list[26], (D, RANK), ((0, 2),), -0.2, 0.2)), 16.384, 409.6),
        "decay_up_square": jnp.clip(jnp.exp(math.log(409.6) - 3.218876 * jax.random.uniform(key_list[27], (RANK, HK), jnp.float32) ** shard_levels(key_list[27], (RANK, HK), ((1, 2),), -0.2, 0.2)), 16.384, 409.6),
        "decay_bias_square": jnp.clip(jnp.exp(math.log(409.6) - 3.218876 * jax.random.uniform(key_list[28], (HK,), jnp.float32) ** shard_levels(key_list[28], (HK,), ((0, 2),), -0.2, 0.2)), 16.384, 409.6),
        "group_gain_square": jnp.clip(jnp.exp(math.log(409.6) - 3.218876 * jax.random.uniform(key_list[29], (VH,), jnp.float32) ** shard_levels(key_list[29], (VH,), ((0, 2),), -0.2, 0.2)), 16.384, 409.6),
        "out_weight_square": jnp.clip(jnp.exp(math.log(409.6) - 3.218876 * jax.random.uniform(key_list[30], (HV, D), jnp.float32) ** shard_levels(key_list[30], (HV, D), ((0, 2),), -0.2, 0.2)), 16.384, 409.6),
        "gate_up_square": jnp.clip(jnp.exp(math.log(409.6) - 3.218876 * jax.random.uniform(key_list[31], (2, D, FF), jnp.float32) ** shard_levels(key_list[31], (2, D, FF), ((1, 2),), -0.2, 0.2)), 16.384, 409.6),
        "down_weight_square": jnp.clip(jnp.exp(math.log(409.6) - 3.218876 * jax.random.uniform(key_list[32], (FF, D), jnp.float32) ** shard_levels(key_list[32], (FF, D), ((0, 2),), -0.2, 0.2)), 16.384, 409.6),
    }


EPS_NORM = 1e-06
EPS_GROUP = 1.0
GATE_NORM = 16.0
LEARN_RATE = 0.005
BETA_ONE = 0.9
BETA_TWO = 0.95
EPS_ADAM = 1e-08
WEIGHT_DECAY = 0.1
PRECISE = lax.Precision.HIGHEST

def product(first_op, second_op):
    return jnp.einsum('ta,ab->tb', first_op, second_op, preferred_element_type=jnp.float32)

def product_tn(first_op, second_op):
    return jnp.einsum('ta,tb->ab', first_op, second_op, preferred_element_type=jnp.float32)

def product_nt(first_op, second_op):
    return jnp.einsum('ta,ba->tb', first_op, second_op, preferred_element_type=jnp.float32)

def rms_forward(values, scaling, epsilon):
    inv_rms = lax.rsqrt(lax.optimization_barrier(jnp.mean(values * values, axis=-1, keepdims=True)) + epsilon)
    return (values * inv_rms * scaling, inv_rms)

def rms_backward(values, inv_rms, scaling, upstream):
    scaled = upstream * scaling
    inner_mean = lax.optimization_barrier(jnp.mean(scaled * values, axis=-1, keepdims=True))
    return inv_rms * (scaled - values * inv_rms * inv_rms * inner_mean)

def swish_grad(values):
    logistic = jax.nn.sigmoid(values)
    return logistic * (1.0 + values * (1.0 - logistic))

def block_masks(labels):
    length = labels.shape[0]
    row_ids = lax.broadcasted_iota(jnp.int32, (length, length), 0)
    col_ids = lax.broadcasted_iota(jnp.int32, (length, length), 1)
    return (labels[:, None] == labels[None, :]) & (row_ids >= col_ids)

def decay_table(cumulative, causal):
    allowed = causal[:, :, None, None]
    spread = cumulative[:, None] - cumulative[None, :]
    return jnp.where(allowed, jnp.exp(jnp.where(allowed, spread, 0.0)), 0.0)

def block_forward(carried, inputs):
    memory, owner_label = carried
    queries, key_rows, values, decays, labels = inputs
    factor = queries.shape[-1] ** (-0.5)
    cumulative = jnp.cumsum(decays, axis=0)
    damping = decay_table(cumulative, block_masks(labels))
    scores = factor * jnp.einsum('tshi,shi->tsh', damping * queries[:, None], key_rows, precision=PRECISE)
    within = jnp.einsum('tsh,shv->thv', scores, values, precision=PRECISE)
    inward = (labels == owner_label)[:, None, None]
    across = factor * jnp.einsum('thi,hiv->thv', queries * jnp.exp(cumulative), memory, precision=PRECISE)
    output = within + jnp.where(inward, across, 0.0)
    last_label = labels[-1]
    tail_decay = jnp.where((labels == last_label)[:, None, None], jnp.exp(cumulative[-1][None] - cumulative), 0.0)
    passed = jnp.where(owner_label == last_label, jnp.exp(cumulative[-1])[:, :, None] * memory, 0.0)
    new_memory = passed + jnp.einsum('shi,shv->hiv', key_rows * tail_decay, values, precision=PRECISE)
    return ((new_memory, last_label), (output, memory, owner_label))

def block_flow(later_grad, inputs):
    queries, decays, labels, grad_out, owner_label = inputs
    factor = queries.shape[-1] ** (-0.5)
    cumulative = jnp.cumsum(decays, axis=0)
    weighted = jnp.where((labels == owner_label)[:, None, None], factor * queries * jnp.exp(cumulative), 0.0)
    earlier_grad = jnp.einsum('thi,thv->hiv', weighted, grad_out, precision=PRECISE)
    earlier_grad = earlier_grad + jnp.where(owner_label == labels[-1], jnp.exp(cumulative[-1])[:, :, None] * later_grad, 0.0)
    return (earlier_grad, later_grad)

def block_grads(inputs):
    queries, key_rows, values, decays, labels, grad_out, before, owner_label, after = inputs
    factor = queries.shape[-1] ** (-0.5)
    cumulative = jnp.cumsum(decays, axis=0)
    damping = decay_table(cumulative, block_masks(labels))
    scores = factor * jnp.einsum('tshi,shi->tsh', damping * queries[:, None], key_rows, precision=PRECISE)
    grad_scores = jnp.einsum('thv,shv->tsh', grad_out, values, precision=PRECISE)
    grad_values = jnp.einsum('tsh,thv->shv', scores, grad_out, precision=PRECISE)
    grad_queries = factor * jnp.einsum('tsh,tshi->thi', grad_scores, damping * key_rows[None], precision=PRECISE)
    grad_keys = factor * jnp.einsum('tsh,tshi->shi', grad_scores, damping * queries[:, None], precision=PRECISE)
    inward = (labels == owner_label)[:, None, None]
    from_state = jnp.einsum('thv,hiv->thi', grad_out, before, precision=PRECISE)
    grad_queries = grad_queries + jnp.where(inward, factor * jnp.exp(cumulative) * from_state, 0.0)
    last_label = labels[-1]
    tail_decay = jnp.where((labels == last_label)[:, None, None], jnp.exp(cumulative[-1][None] - cumulative), 0.0)
    grad_keys = grad_keys + tail_decay * jnp.einsum('shv,hiv->shi', values, after, precision=PRECISE)
    grad_values = grad_values + jnp.einsum('shi,hiv->shv', key_rows * tail_decay, after, precision=PRECISE)
    return (grad_queries, grad_keys, grad_values)

def block_suffix(carried, inputs):
    running_sum, next_label = carried
    summands, labels = inputs
    length = labels.shape[0]
    row_ids = lax.broadcasted_iota(jnp.int32, (length, length), 0)
    col_ids = lax.broadcasted_iota(jnp.int32, (length, length), 1)
    later_mask = ((labels[:, None] == labels[None, :]) & (col_ids >= row_ids)).astype(jnp.float32)
    inside = jnp.einsum('ts,shi->thi', later_mask, summands, precision=PRECISE)
    inside = inside + jnp.where((labels == next_label)[:, None, None], running_sum[None], 0.0)
    first_label = labels[0]
    head_sum = lax.optimization_barrier(jnp.sum(jnp.where((labels == first_label)[:, None, None], summands, 0.0), axis=0))
    head_sum = head_sum + jnp.where(first_label == next_label, running_sum, 0.0)
    return ((head_sum, first_label), inside)

def adamw_update(weight, gradient, moment_one, moment_two):
    new_first = BETA_ONE * moment_one + (1.0 - BETA_ONE) * gradient
    new_second = BETA_TWO * moment_two + (1.0 - BETA_TWO) * gradient * gradient
    correct_one = 1.0 - BETA_ONE ** ADAM_STEP
    correct_two = 1.0 - BETA_TWO ** ADAM_STEP
    direction = new_first / correct_one / (jnp.sqrt(new_second / correct_two) + EPS_ADAM)
    return (weight - LEARN_RATE * (direction + WEIGHT_DECAY * weight), new_first, new_second)

def one_sequence(lowered, token_in, label_ints, cot_in):
    norm_all, query_mats, value_mats, down_rank, up_rank, bias_all, group_all, out_mats, gate_mats, down_mats = lowered
    token_rows = token_in.astype(jnp.bfloat16)
    cot_rows = cot_in.astype(jnp.bfloat16)
    inputs_f = token_rows.astype(jnp.float32)
    labels = label_ints.astype(jnp.float32)
    length = inputs_f.shape[0]
    blocks = length // BLOCK
    gain_one = norm_all[0].astype(jnp.float32)
    gain_two = norm_all[1].astype(jnp.float32)
    normed_f, rstd_one = rms_forward(inputs_f, gain_one, EPS_NORM)
    normed = normed_f.astype(jnp.bfloat16)
    queries = product(normed, query_mats[0]).astype(jnp.bfloat16)
    key_rows = product(normed, query_mats[1]).astype(jnp.bfloat16)
    values = product(normed, value_mats[0]).astype(jnp.bfloat16)
    out_gate = product(normed, value_mats[1])
    lowrank = product(normed, down_rank).astype(jnp.bfloat16)
    logits = product(lowrank, up_rank) + bias_all.astype(jnp.float32)
    log_decay = jax.nn.log_sigmoid(logits) / GATE_NORM
    query_blocks = queries.astype(jnp.float32).reshape(blocks, BLOCK, HEADS, KH)
    key_blocks = key_rows.astype(jnp.float32).reshape(blocks, BLOCK, HEADS, KH)
    value_blocks = values.astype(jnp.float32).reshape(blocks, BLOCK, HEADS, VH)
    decay_blocks = log_decay.reshape(blocks, BLOCK, HEADS, KH)
    label_blocks = labels.reshape(blocks, BLOCK)
    empty_state = jnp.zeros((HEADS, KH, VH), jnp.float32)
    start_label = jnp.full((), -1.0, jnp.float32)
    _, (mixer_blocks, before_states, owners) = lax.scan(block_forward, (empty_state, start_label), (query_blocks, key_blocks, value_blocks, decay_blocks, label_blocks))
    mixer_out = mixer_blocks.reshape(length, HEADS, VH)
    group_rstd = lax.rsqrt(lax.optimization_barrier(jnp.mean(mixer_out * mixer_out, axis=-1, keepdims=True)) + EPS_GROUP)
    group_gain_f = group_all.astype(jnp.float32)
    group_normed = mixer_out * group_rstd * group_gain_f
    gate_heads = out_gate.reshape(length, HEADS, VH)
    swished = gate_heads * jax.nn.sigmoid(gate_heads)
    mixer_low = (group_normed * swished).reshape(length, HEADS * VH).astype(jnp.bfloat16)
    residual = inputs_f + product(mixer_low, out_mats)
    normed_two_f, rstd_two = rms_forward(residual, gain_two, EPS_NORM)
    normed_two = normed_two_f.astype(jnp.bfloat16)
    gate_pre = product(normed_two, gate_mats[0])
    up_pre = product(normed_two, gate_mats[1])
    hidden = (jax.nn.silu(gate_pre) * up_pre).astype(jnp.bfloat16)
    output = (residual + product(hidden, down_mats)).astype(jnp.bfloat16)
    grad_down = product_tn(hidden, cot_rows)
    grad_hidden = product_nt(cot_rows, down_mats)
    grad_gate = (grad_hidden * up_pre * swish_grad(gate_pre)).astype(jnp.bfloat16)
    grad_upper = (grad_hidden * jax.nn.silu(gate_pre)).astype(jnp.bfloat16)
    grad_gate_up = jnp.stack([product_tn(normed_two, grad_gate), product_tn(normed_two, grad_upper)])
    grad_normed_two = product_nt(grad_gate, gate_mats[0]) + product_nt(grad_upper, gate_mats[1])
    grad_gain_two = lax.optimization_barrier(jnp.sum(grad_normed_two * residual * rstd_two, axis=0))
    grad_residual = cot_rows.astype(jnp.float32) + rms_backward(residual, rstd_two, gain_two, grad_normed_two)
    grad_res_low = grad_residual.astype(jnp.bfloat16)
    grad_out = product_tn(mixer_low, grad_res_low)
    grad_mixed = product_nt(grad_res_low, out_mats).reshape(length, HEADS, VH)
    grad_group_normed = grad_mixed * swished
    grad_gate_heads = grad_mixed * group_normed * swish_grad(gate_heads)
    grad_group_gain = lax.optimization_barrier(jnp.sum(grad_group_normed * mixer_out * group_rstd, axis=(0, 1)))
    grad_attn = rms_backward(mixer_out, group_rstd, group_gain_f, grad_group_normed).astype(jnp.bfloat16)
    grad_blocks = grad_attn.astype(jnp.float32).reshape(blocks, BLOCK, HEADS, VH)
    _, after_states = lax.scan(block_flow, empty_state, (query_blocks, decay_blocks, label_blocks, grad_blocks, owners), reverse=True)
    grad_query_b, grad_key_b, grad_value_b = lax.map(block_grads, (query_blocks, key_blocks, value_blocks, decay_blocks, label_blocks, grad_blocks, before_states, owners, after_states))
    summands = query_blocks * grad_query_b - key_blocks * grad_key_b
    _, grad_log = lax.scan(block_suffix, (jnp.zeros((HEADS, KH), jnp.float32), start_label), (summands, label_blocks), reverse=True)
    grad_logits = grad_log.reshape(length, HEADS * KH) * jax.nn.sigmoid(-logits) / GATE_NORM
    grad_logits_low = grad_logits.astype(jnp.bfloat16)
    grad_bias = lax.optimization_barrier(jnp.sum(grad_logits, axis=0))
    grad_up_rank = product_tn(lowrank, grad_logits_low)
    grad_low = product_nt(grad_logits_low, up_rank).astype(jnp.bfloat16)
    grad_down_rank = product_tn(normed, grad_low)
    grad_query_low = grad_query_b.reshape(length, HEADS * KH).astype(jnp.bfloat16)
    grad_keys_low = grad_key_b.reshape(length, HEADS * KH).astype(jnp.bfloat16)
    grad_values_low = grad_value_b.reshape(length, HEADS * VH).astype(jnp.bfloat16)
    grad_gate_low = grad_gate_heads.reshape(length, HEADS * VH).astype(jnp.bfloat16)
    grad_query_key = jnp.stack([product_tn(normed, grad_query_low), product_tn(normed, grad_keys_low)])
    grad_value_gate = jnp.stack([product_tn(normed, grad_values_low), product_tn(normed, grad_gate_low)])
    grad_normed = product_nt(grad_query_low, query_mats[0]) + product_nt(grad_keys_low, query_mats[1])
    grad_normed = grad_normed + product_nt(grad_values_low, value_mats[0]) + product_nt(grad_gate_low, value_mats[1])
    grad_normed = grad_normed + product_nt(grad_low, down_rank)
    grad_gain_one = lax.optimization_barrier(jnp.sum(grad_normed * inputs_f * rstd_one, axis=0))
    grad_tokens = (grad_residual + rms_backward(inputs_f, rstd_one, gain_one, grad_normed)).astype(jnp.bfloat16)
    gradients = (jnp.stack([grad_gain_one, grad_gain_two]), grad_query_key, grad_value_gate, grad_down_rank, grad_up_rank, grad_bias, grad_group_gain, grad_out, grad_gate_up, grad_down)
    return (output, grad_tokens, gradients)

def reference(tokens, segment_ids, cotangent, norm_gains, query_key, value_gate, decay_down, decay_up, decay_bias, group_gain, out_weight, gate_up, down_weight, norm_gains_mean, query_key_mean, value_gate_mean, decay_down_mean, decay_up_mean, decay_bias_mean, group_gain_mean, out_weight_mean, gate_up_mean, down_weight_mean, norm_gains_square, query_key_square, value_gate_square, decay_down_square, decay_up_square, decay_bias_square, group_gain_square, out_weight_square, gate_up_square, down_weight_square):
    masters = (norm_gains, query_key, value_gate, decay_down, decay_up, decay_bias, group_gain, out_weight, gate_up, down_weight)
    first_moments = (norm_gains_mean, query_key_mean, value_gate_mean, decay_down_mean, decay_up_mean, decay_bias_mean, group_gain_mean, out_weight_mean, gate_up_mean, down_weight_mean)
    second_moments = (norm_gains_square, query_key_square, value_gate_square, decay_down_square, decay_up_square, decay_bias_square, group_gain_square, out_weight_square, gate_up_square, down_weight_square)
    lowered = tuple((weight.astype(jnp.bfloat16) for weight in masters))

    def accumulate(totals, inputs):
        token_rows, label_rows, cot_rows = inputs
        output, grad_rows, gradients = one_sequence(lowered, token_rows, label_rows, cot_rows)
        return (tuple((running + adding.astype(jnp.float32) for running, adding in zip(totals, gradients))), (output, grad_rows))
    zeros_init = tuple((jnp.zeros(weight.shape, jnp.float32) for weight in masters))
    gradients, (outputs, grad_tokens) = lax.scan(accumulate, zeros_init, (tokens, segment_ids, cotangent))
    updated = tuple((adamw_update(masters[number].astype(jnp.float32), gradients[number], first_moments[number].astype(jnp.float32), second_moments[number].astype(jnp.float32)) for number in range(10)))
    return (outputs, grad_tokens, gradients[0], gradients[1], gradients[2], gradients[3], gradients[4], gradients[5], gradients[6], gradients[7], gradients[8], gradients[9], updated[0][0], updated[1][0], updated[2][0], updated[3][0], updated[4][0], updated[5][0], updated[6][0], updated[7][0], updated[8][0], updated[9][0], updated[0][1], updated[1][1], updated[2][1], updated[3][1], updated[4][1], updated[5][1], updated[6][1], updated[7][1], updated[8][1], updated[9][1], updated[0][2], updated[1][2], updated[2][2], updated[3][2], updated[4][2], updated[5][2], updated[6][2], updated[7][2], updated[8][2], updated[9][2])
```

```python
import functools

import jax
import jax.numpy as jnp
from jax import lax
from jax.experimental import pallas as pl
from jax.experimental.pallas import tpu as pltpu
from jax.sharding import PartitionSpec as P

HEADS = 2
KH = 128
VH = 256
ADAM_STEP = 3
EPS_NORM = 1e-06
EPS_GROUP = 1.0
GATE_NORM = 16.0
LEARN_RATE = 0.005
BETA_ONE = 0.9
BETA_TWO = 0.95
EPS_ADAM = 1e-08
WEIGHT_DECAY = 0.1
PRECISE = lax.Precision.HIGHEST
F32 = jnp.float32
BF16 = jnp.bfloat16
FACTOR = KH ** (-0.5)
ROWS = 64
TOP = 80.0


def dot(a, b, precision=None):
    return lax.dot_general(a, b, (((1,), (0,)), ((), ())), precision=precision, preferred_element_type=F32)


def dot_nt(a, b, precision=None):
    return lax.dot_general(a, b, (((1,), (1,)), ((), ())), precision=precision, preferred_element_type=F32)


def dot_tn(a, b, precision=None):
    return lax.dot_general(a, b, (((0,), (0,)), ((), ())), precision=precision, preferred_element_type=F32)


def logistic(v):
    return 1.0 / (1.0 + jnp.exp(-v))


class Pieces:
    def __init__(self, parts, shape):
        self.arrays = tuple(a for a, _ in parts)
        self.places = tuple(f for _, f in parts)
        self.shape = shape


def copies_of(pieces, refs, scratch, sems, idx):
    out = []
    for n, (ref, place) in enumerate(zip(refs, pieces.places)):
        rows = ref.shape[0]
        at = pl.multiple_of(place(idx), 16)
        out.append(pltpu.make_async_copy(ref, scratch.at[pl.ds(at, rows)], sems.at[n]))
    return out


def call(body, idx, acts, weights, outs):
    n_act = len(acts)
    counts = [len(w.arrays) for w in weights]

    def kernel(*refs):
        idx_ref = refs[0]
        act_refs = refs[1 : 1 + n_act]
        at = 1 + n_act
        weight_refs = []
        for n in counts:
            weight_refs.append(refs[at : at + n])
            at += n
        out_refs = refs[at : at + len(outs)]
        at += len(outs)
        loaders = []
        for j, w in enumerate(weights):
            scratch, sems = refs[at + 2 * j], refs[at + 2 * j + 1]
            started = copies_of(w, weight_refs[j], scratch, sems, idx_ref)
            for cp in started:
                cp.start()

            def load(started=started, scratch=scratch):
                for cp in started:
                    cp.wait()
                return scratch

            loaders.append(load)
        body(idx_ref, act_refs, loaders, out_refs)

    scratch_shapes = []
    for w, n in zip(weights, counts):
        scratch_shapes += [pltpu.VMEM(w.shape, BF16), pltpu.SemaphoreType.DMA((n,))]
    vmem = pl.BlockSpec(memory_space=pltpu.VMEM)
    anyspace = pl.BlockSpec(memory_space=pl.ANY)
    return pl.pallas_call(
        kernel,
        in_specs=[pl.BlockSpec(memory_space=pltpu.SMEM)] + [vmem] * n_act + [anyspace] * sum(counts),
        out_specs=[vmem] * len(outs),
        out_shape=[jax.ShapeDtypeStruct(s, d) for s, d in outs],
        scratch_shapes=scratch_shapes,
        compiler_params=pltpu.CompilerParams(vmem_limit_bytes=56 << 20),
        name=body.__name__,
    )(idx, *acts, *[a for w in weights for a in w.arrays])


def heads(h):
    return slice(h * KH, (h + 1) * KH), slice(h * VH, (h + 1) * VH)


def allowed_mask(lab_c, lab_r):
    shape = (lab_c.shape[0], lab_r.shape[1])
    rows = lax.broadcasted_iota(jnp.int32, shape, 0)
    cols = lax.broadcasted_iota(jnp.int32, shape, 1)
    return (lab_c == lab_r) & (rows >= cols)


def project(idx, acts, loaders, outs):
    x, gains, lab_c, down_rank, up_rank, bias = acts
    normed_o, q_o, k_o, v_o, gate_o, low_o, logits_o, cum_o, msg_o = outs
    xf = x[...].astype(F32)
    r_one = lax.rsqrt(jnp.mean(xf * xf, axis=-1, keepdims=True) + EPS_NORM)
    normed = (xf * r_one * gains[0:1, :].astype(F32)).astype(BF16)
    normed_o[...] = normed
    low = dot(normed, down_rank[...]).astype(BF16)
    low_o[...] = low
    logits = dot(low, up_rank[...]) + bias[...].astype(F32)
    logits_o[...] = logits
    log_decay = (jnp.minimum(logits, 0.0) - jnp.log1p(jnp.exp(-jnp.abs(logits)))) / GATE_NORM
    length = xf.shape[0]
    rows = lax.broadcasted_iota(jnp.int32, (length, length), 0)
    cols = lax.broadcasted_iota(jnp.int32, (length, length), 1)
    lower = jnp.where(rows >= cols, 1.0, 0.0).astype(F32)
    cum = dot(lower, log_decay, PRECISE)
    cum_o[...] = cum
    total = dot_tn(log_decay, jnp.ones((length, 128), F32), PRECISE)
    msg_o[:, VH:] = jnp.where(idx[5] > 0, jnp.exp(total), 0.0).astype(BF16)
    weights = loaders[0]()
    width = HEADS * KH
    q_o[...] = dot(normed, weights[:, :width]).astype(BF16)
    keys = dot(normed, weights[:, width : 2 * width]).astype(BF16)
    k_o[...] = keys
    values = dot(normed, weights[:, 2 * width : 2 * width + HEADS * VH]).astype(BF16)
    v_o[...] = values
    gate_o[...] = dot(normed, weights[:, 2 * width + HEADS * VH :])
    tail = jnp.where(lab_c[...] == idx[3], jnp.exp(cum[length - 1 : length] - cum), 0.0)
    ending = (keys.astype(F32) * tail).astype(BF16)
    for h in range(HEADS):
        ks, vs = heads(h)
        msg_o[ks, :VH] = dot_tn(ending[:, ks], values[:, vs]).astype(BF16)


def scaled_block(q, k, cum, ks, b, length):
    lo, hi = b * ROWS, (b + 1) * ROWS
    reach = min(length, -(-hi // 128) * 128)
    middle = cum[lo + ROWS // 2 : lo + ROWS // 2 + 1, ks]
    rise = jnp.exp(jnp.minimum(cum[lo:hi, ks] - middle, TOP))
    fall = jnp.exp(jnp.minimum(middle - cum[:reach, ks], TOP))
    q_part = (q[lo:hi, ks].astype(F32) * rise).astype(BF16)
    k_part = (k[:reach, ks].astype(F32) * fall).astype(BF16)
    return lo, hi, reach, rise, fall, q_part, k_part


def within(idx, acts, loaders, outs):
    q, k, v, cum, lab_c, lab_r = acts
    scores_o, local_o = outs
    length = q.shape[0]
    allowed = allowed_mask(lab_c[...], lab_r[...])
    for h in range(HEADS):
        ks, vs = heads(h)
        for b in range(length // ROWS):
            lo, hi, reach, _, _, q_part, k_part = scaled_block(q, k, cum, ks, b, length)
            block = jnp.where(allowed[lo:hi, :reach], FACTOR * dot_nt(q_part, k_part), 0.0)
            scores_o[h, lo:hi, :reach] = block.astype(BF16)
            if reach < length:
                scores_o[h, lo:hi, reach:] = jnp.zeros((hi - lo, length - reach), BF16)
        local_o[:, vs] = dot(scores_o[h], v[:, vs])


def entering(idx, q, cum, lab_c):
    head_rows = (lab_c[...] == idx[2]) & (idx[4] > 0)
    rising = jnp.where(head_rows, FACTOR * jnp.exp(cum[...]), 0.0)
    return rising, (q[...].astype(F32) * rising).astype(BF16)


def forward_rest(idx, acts, loaders, outs):
    x, local, q, cum, lab_c, out_gate, near, far, gains, group_gain = acts
    attn_o, mixed_o, res_o, n2_o, gu_o, hidden_o, out_o, state_o = outs
    state = near[:, :VH].astype(F32) + near[:, VH : VH + 1].astype(F32) * far[:, :VH].astype(F32)
    state_o[...] = state
    state_low = state.astype(BF16)
    _, entry = entering(idx, q, cum, lab_c)
    gain = group_gain[...].astype(F32)
    for h in range(HEADS):
        ks, vs = heads(h)
        attn = local[:, vs] + dot(entry[:, ks], state_low[ks, :])
        attn_o[:, vs] = attn
        g = lax.rsqrt(jnp.mean(attn * attn, axis=-1, keepdims=True) + EPS_GROUP)
        gate = out_gate[:, vs]
        mixed_o[:, vs] = (attn * g * gain * (gate * logistic(gate))).astype(BF16)
    out_w = loaders[0]()
    res = x[...].astype(F32) + dot(mixed_o[...], out_w[...])
    res_o[...] = res
    r_two = lax.rsqrt(jnp.mean(res * res, axis=-1, keepdims=True) + EPS_NORM)
    n2 = (res * r_two * gains[1:2, :].astype(F32)).astype(BF16)
    n2_o[...] = n2
    gu_w = loaders[1]()
    width = hidden_o.shape[1]
    gate = dot(n2, gu_w[:, :width])
    gu_o[:, :width] = gate
    upper = dot(n2, gu_w[:, width:])
    gu_o[:, width:] = upper
    hidden_o[...] = (gate * logistic(gate) * upper).astype(BF16)
    down_w = loaders[2]()
    out_o[...] = (res + dot(hidden_o[...], down_w[...])).astype(BF16)


def backward_ffn(idx, acts, loaders, outs):
    cot, gu, res, attn, q, cum, lab_c, out_gate, gains, group_gain, msg = acts
    pair_o, gres_o, glow_o, gog_o, ga_o, flow_o, gain_o, ggroup_o = outs
    width = gu.shape[1] // 2
    down_w = loaders[0]()
    grad_hidden = dot_nt(cot[...], down_w[...])
    gate = gu[:, :width]
    s = logistic(gate)
    pair_o[:, :width] = (grad_hidden * gu[:, width:] * (s * (1.0 + gate * (1.0 - s)))).astype(BF16)
    pair_o[:, width:] = (grad_hidden * (gate * s)).astype(BF16)
    gu_w = loaders[1]()
    gn2 = dot_nt(pair_o[...], gu_w[...])
    rf = res[...]
    r_two = lax.rsqrt(jnp.mean(rf * rf, axis=-1, keepdims=True) + EPS_NORM)
    gain_o[...] = jnp.sum(gn2 * (rf * r_two), axis=0, keepdims=True)
    u = gn2 * gains[1:2, :].astype(F32)
    inner = jnp.mean(u * rf, axis=-1, keepdims=True)
    gres = cot[...].astype(F32) + r_two * (u - rf * (r_two * r_two * inner))
    gres_o[...] = gres
    low = gres.astype(BF16)
    glow_o[...] = low
    out_w = loaders[2]()
    gmix = dot_nt(low, out_w[...])
    gain = group_gain[...].astype(F32)
    _, entry = entering(idx, q, cum, lab_c)
    ggroup = jnp.zeros((1, VH), F32)
    for h in range(HEADS):
        ks, vs = heads(h)
        at = attn[:, vs]
        g = lax.rsqrt(jnp.mean(at * at, axis=-1, keepdims=True) + EPS_GROUP)
        og = out_gate[:, vs]
        so = logistic(og)
        gm = gmix[:, vs]
        gog_o[:, vs] = (gm * (at * g * gain) * (so * (1.0 + og * (1.0 - so)))).astype(BF16)
        ggn = gm * (og * so)
        ggroup = ggroup + jnp.sum(ggn * (at * g), axis=0, keepdims=True)
        ug = ggn * gain
        mean = jnp.mean(ug * at, axis=-1, keepdims=True)
        ga = (g * (ug - at * (g * g * mean))).astype(BF16)
        ga_o[:, vs] = ga
        flow_o[ks, :VH] = dot_tn(entry[:, ks], ga).astype(BF16)
    ggroup_o[...] = ggroup
    flow_o[:, VH:] = msg[:, VH:]


def backward_within(idx, acts, loaders, outs):
    q, k, v, cum, lab_c, lab_r, scores, ga = acts
    dq_o, dk_o, dv_o = outs
    length = q.shape[0]
    allowed = allowed_mask(lab_c[...], lab_r[...])
    for h in range(HEADS):
        ks, vs = heads(h)
        dv_o[:, vs] = dot_tn(scores[h], ga[:, vs])
        dscore = jnp.where(allowed, FACTOR * dot_nt(ga[:, vs], v[:, vs]), 0.0).astype(BF16)
        dk = None
        for b in reversed(range(length // ROWS)):
            lo, hi, reach, rise, fall, q_part, k_part = scaled_block(q, k, cum, ks, b, length)
            part = dscore[lo:hi, :reach]
            dq_o[lo:hi, ks] = dot(part, k_part) * rise
            more = dot_tn(part, q_part) * fall
            if dk is None:
                dk_o[:, ks] = more
                dk = True
            else:
                dk_o[:reach, ks] += more


def backward_rest(idx, acts, loaders, outs):
    x, q, k, v, cum, lab_c, lab_r, logits, low, ga, gog, gres, state, msg, near, far, dq, dk, dv, gains, down_rank, up_rank = acts
    cat_o, gtok_o, gain_o, gbias_o, gup_o = outs
    length = q.shape[0]
    flow = near[:, :VH].astype(F32) + near[:, VH : VH + 1].astype(F32) * far[:, :VH].astype(F32)
    flow_low = flow.astype(BF16)
    st = state[...]
    st_low = st.astype(BF16)
    end = msg[:, :VH].astype(F32) + msg[:, VH : VH + 1].astype(F32) * st
    beyond = dot_nt(jnp.ones((length, VH), F32), end * flow, PRECISE)
    cumv = cum[...]
    rising, _ = entering(idx, q, cum, lab_c)
    ends = lab_c[...] == idx[3]
    tail = jnp.where(ends, jnp.exp(cumv[length - 1 : length] - cumv), 0.0)
    kf = k[...].astype(F32)
    qf = q[...].astype(F32)
    ending = (kf * tail).astype(BF16)
    width = HEADS * KH
    gqs, gks = [], []
    for h in range(HEADS):
        ks, vs = heads(h)
        gq = dq[:, ks] + rising[:, ks] * dot_nt(ga[:, vs], st_low[ks, :])
        gk = dk[:, ks] + tail[:, ks] * dot_nt(v[:, vs], flow_low[ks, :])
        gv = dv[:, vs] + dot(ending[:, ks], flow_low[ks, :])
        cat_o[:, ks] = gq.astype(BF16)
        cat_o[:, slice(width + h * KH, width + (h + 1) * KH)] = gk.astype(BF16)
        cat_o[:, slice(2 * width + h * VH, 2 * width + (h + 1) * VH)] = gv.astype(BF16)
        gqs.append(qf[:, ks] * gq - kf[:, ks] * gk)
    base = 2 * width + HEADS * VH
    cat_o[:, base : base + HEADS * VH] = gog[...]
    summands = jnp.concatenate(gqs, axis=1)
    rows = lax.broadcasted_iota(jnp.int32, (length, length), 0)
    cols = lax.broadcasted_iota(jnp.int32, (length, length), 1)
    later = jnp.where((lab_c[...] == lab_r[...]) & (cols >= rows), 1.0, 0.0).astype(F32)
    glog = dot(later, summands, PRECISE) + jnp.where(ends, beyond, 0.0)
    lg = logits[...]
    glogits = glog * logistic(-lg) / GATE_NORM
    gbias_o[...] = jnp.sum(glogits, axis=0, keepdims=True)
    gll = glogits.astype(BF16)
    gup_o[...] = dot_tn(low[...], gll)
    glow = dot_nt(gll, up_rank[...]).astype(BF16)
    base = base + HEADS * VH
    rank = glow.shape[1]
    cat_o[:, base:] = jnp.zeros((length, cat_o.shape[1] - base), BF16)
    cat_o[:, base : base + rank] = glow
    weights = loaders[0]()
    gn = dot_nt(cat_o[:, :base], weights[...]) + dot_nt(glow, down_rank[...])
    xf = x[...].astype(F32)
    r_one = lax.rsqrt(jnp.mean(xf * xf, axis=-1, keepdims=True) + EPS_NORM)
    gain_o[...] = jnp.sum(gn * (xf * r_one), axis=0, keepdims=True)
    u = gn * gains[0:1, :].astype(F32)
    inner = jnp.mean(u * xf, axis=-1, keepdims=True)
    gtok_o[...] = (gres[...] + r_one * (u - xf * (r_one * r_one * inner))).astype(BF16)


def adamw_update(weight, gradient, moment_one, moment_two):
    new_first = BETA_ONE * moment_one + (1.0 - BETA_ONE) * gradient
    new_second = BETA_TWO * moment_two + (1.0 - BETA_TWO) * gradient * gradient
    correct_one = 1.0 - BETA_ONE**ADAM_STEP
    correct_two = 1.0 - BETA_TWO**ADAM_STEP
    direction = new_first / correct_one / (jnp.sqrt(new_second / correct_two) + EPS_ADAM)
    return (weight - LEARN_RATE * (direction + WEIGHT_DECAY * weight), new_first, new_second)


def swap(bit, size):
    return [(a, a ^ bit) for a in range(size)]


def over_x(v):
    return lax.ppermute(v, "fsdp", swap(1, 2))


def over_core(v):
    return lax.ppermute(v, "seq", swap(1, 4))


def over_y(v):
    return lax.ppermute(v, "seq", swap(2, 4))


def over_z(v, bit):
    return lax.ppermute(v, "rep", swap(bit, 4))


def half_of(v, axis, which):
    size = v.shape[axis] // 2
    return lax.dynamic_slice_in_dim(v, which * size, size, axis)


def joined(own, other, axis, bit):
    return jnp.where(bit == 0, jnp.concatenate([own, other], axis), jnp.concatenate([other, own], axis))


def add_low(a, b):
    return (a.astype(F32) + b.astype(F32)).astype(BF16)


def reduced(part_of, y_axis, z_axis):
    i, p, r = lax.axis_index("fsdp"), lax.axis_index("seq"), lax.axis_index("rep")
    core, y, z0, z1 = p % 2, p // 2, r % 2, r // 2
    got = over_core(part_of(1 - core).astype(BF16))
    kept = add_low(part_of(core), got)
    got = over_x(lax.dynamic_index_in_dim(kept, 1 - i, 0, False))
    a = add_low(lax.dynamic_index_in_dim(kept, i, 0, False), got)
    got = over_y(half_of(a, y_axis, 1 - y))
    a = add_low(half_of(a, y_axis, y), got)
    got = over_z(half_of(a, z_axis, 1 - z0), 1)
    a = add_low(half_of(a, z_axis, z0), got)
    got = over_z(half_of(a, z_axis, 1 - z1), 2)
    a = add_low(half_of(a, z_axis, z1), got)
    a = joined(a, over_z(a, 2), z_axis, z1)
    a = joined(a, over_z(a, 1), z_axis, z0)
    a = joined(a, over_y(a), y_axis, y)
    return a, over_core(a)


def shards(fast, tokens, segment_ids, cotangent, *params):
    masters, firsts, seconds = params[:10], params[10:20], params[20:30]
    norm_gains, query_key, value_gate, decay_down, decay_up, decay_bias, group_gain, out_weight, gate_up, down_weight = masters
    fsdp = lax.axis_size("fsdp")
    seq = lax.axis_size("seq")
    i, p = lax.axis_index("fsdp"), lax.axis_index("seq")
    x = tokens[0]
    cot = cotangent[0]
    labels = segment_ids[0]
    length, width = x.shape
    core = p % 2

    edges = jnp.broadcast_to(labels[length - 1] + 1, (8, 128))
    last_before = lax.ppermute(edges, "seq", [(a, a + 1) for a in range(seq - 1)])[0, 0]
    first, last = labels[0], labels[length - 1]
    linked = (last_before == first + 1).astype(jnp.int32)
    whole = linked * (first == last).astype(jnp.int32)
    idx = jnp.stack([i, p, first, last, linked, whole]).astype(jnp.int32)
    lab_c = labels[:, None]
    lab_r = labels[None, :]

    own_q = jnp.concatenate([query_key[0], query_key[1], value_gate[0], value_gate[1]], axis=1).astype(BF16)
    own_gu = jnp.concatenate([gate_up[0], gate_up[1]], axis=1).astype(BF16)
    own_out = out_weight.astype(BF16)
    own_down = down_weight.astype(BF16)
    smalls = [norm_gains, decay_down, decay_up, decay_bias, group_gain]
    if fast:
        pack = jnp.concatenate([s.reshape(-1) for s in smalls]).astype(BF16).reshape(-1, 128)
        pack = jnp.pad(pack, ((0, -pack.shape[0] % 16), (0, 0)))
        other = over_x(pack).reshape(-1)
        pack = pack.reshape(-1)
        both = jnp.where(i == 0, jnp.stack([pack, other]), jnp.stack([other, pack]))
        full, at = [], 0
        for s, axis in zip(smalls, (1, 0, 1, 0, 0)):
            n = s.size
            full.append(jnp.concatenate([both[0, at : at + n].reshape(s.shape), both[1, at : at + n].reshape(s.shape)], axis))
            at += n
        gains, down_rank, up_rank, bias, group = full

        def gathered(own, quarters):
            rows, cols = own.shape
            if quarters:
                part = rows // 4
                a = over_x(lax.dynamic_slice_in_dim(own, p * part, part, 0))
                b = over_y(a)
                pieces = [(a, 0), (over_core(a), 1), (b, 2), (over_core(b), 3)]
            else:
                part = rows // 2
                a = over_x(lax.dynamic_slice_in_dim(own, core * part, part, 0))
                pieces = [(a, 0), (over_core(a), 1)]
            parts = [(own, lambda s: s[0] * rows)]
            for array, turn in pieces:
                if quarters:
                    parts.append((array, lambda s, turn=turn: (1 - s[0]) * rows + (s[1] ^ turn) * part))
                else:
                    parts.append((array, lambda s, turn=turn: (1 - s[0]) * rows + ((s[1] % 2) ^ turn) * part))
            return Pieces(parts, (2 * rows, cols))

        w_q = gathered(own_q, False)
        w_out = gathered(own_out, True)
        w_gu = gathered(own_gu, True)
        w_down = gathered(own_down, True)
    else:
        gains, down_rank, up_rank, bias, group = [
            lax.all_gather(s.astype(BF16), "fsdp", axis=axis, tiled=True) for s, axis in zip(smalls, (1, 0, 1, 0, 0))
        ]

        def gathered(own):
            rows, cols = own.shape
            return Pieces([(lax.all_gather(own, "fsdp", axis=0, tiled=True), lambda s: s[0] * 0)], (fsdp * rows, cols))

        w_q, w_out, w_gu, w_down = gathered(own_q), gathered(own_out), gathered(own_gu), gathered(own_down)
    bias = bias[None]
    group = group[None]
    hk, hv = HEADS * KH, HEADS * VH
    ff = w_down.shape[0]

    normed, q, k, v, out_gate, low, logits, cum, msg = call(
        project,
        idx,
        (x, gains, lab_c, down_rank, up_rank, bias),
        (w_q,),
        [((length, width), BF16), ((length, hk), BF16), ((length, hk), BF16), ((length, hv), BF16), ((length, hv), F32),
         ((length, decay_down.shape[1]), BF16), ((length, hk), F32), ((length, hk), F32), ((hk, VH + 128), BF16)],
    )
    near = lax.ppermute(msg, "seq", [(a, a + 1) for a in range(seq - 1)])
    far = lax.ppermute(msg, "seq", [(a, a + 2) for a in range(seq - 2)])
    scores, local = call(
        within, idx, (q, k, v, cum, lab_c, lab_r), (), [((HEADS, length, length), BF16), ((length, hv), F32)]
    )
    attn, mixed, residual, normed_two, gu, hidden, output, state = call(
        forward_rest,
        idx,
        (x, local, q, cum, lab_c, out_gate, near, far, gains, group),
        (w_out, w_gu, w_down),
        [((length, hv), F32), ((length, hv), BF16), ((length, width), F32), ((length, width), BF16), ((length, 2 * ff), F32),
         ((length, ff), BF16), ((length, width), BF16), ((hk, VH), F32)],
    )
    pair, gres, gres_low, gog, ga, flow, gain_two, ggroup = call(
        backward_ffn,
        idx,
        (cot, gu, residual, attn, q, cum, lab_c, out_gate, gains, group, msg),
        (w_down, w_gu, w_out),
        [((length, 2 * ff), BF16), ((length, width), F32), ((length, width), BF16), ((length, hv), BF16), ((length, hv), BF16),
         ((hk, VH + 128), BF16), ((1, width), F32), ((1, VH), F32)],
    )
    near_flow = lax.ppermute(flow, "seq", [(a + 1, a) for a in range(seq - 1)])
    far_flow = lax.ppermute(flow, "seq", [(a + 2, a) for a in range(seq - 2)])
    dq, dk, dv = call(
        backward_within, idx, (q, k, v, cum, lab_c, lab_r, scores, ga), (),
        [((length, hk), F32), ((length, hk), F32), ((length, hv), F32)],
    )
    rank = decay_down.shape[1]
    cat_width = -(-(2 * hk + 2 * hv + rank) // 128) * 128
    cat, grad_tokens, gain_one, gbias, gup = call(
        backward_rest,
        idx,
        (x, q, k, v, cum, lab_c, lab_r, logits, low, ga, gog, gres, state, msg, near_flow, far_flow, dq, dk, dv, gains, down_rank, up_rank),
        (w_q,),
        [((length, cat_width), BF16), ((length, width), BF16), ((1, width), F32), ((1, hk), F32), ((rank, hk), F32)],
    )

    def split_q(g):
        gq, gk, gv, gg = g[:, :hk], g[:, hk : 2 * hk], g[:, 2 * hk : 2 * hk + hv], g[:, 2 * hk + hv : 2 * hk + 2 * hv]
        return jnp.stack([gq, gk]), jnp.stack([gv, gg]), g[:, 2 * hk + 2 * hv : 2 * hk + 2 * hv + rank]

    small_grads = [jnp.concatenate([gain_one, gain_two]), gup, gbias[0], ggroup[0]]
    small_axes = (1, 1, 0, 0)
    if fast:
        def rows_of(act, grad):
            shaped = act.reshape(length, 2, 2, act.shape[1] // 4)

            def part_of(kk):
                chosen = lax.dynamic_index_in_dim(shaped, kk, 2, False)
                return jnp.einsum("thr,tn->hrn", chosen, grad, preferred_element_type=F32)

            return part_of

        def cols_of(act, grad):
            def part_of(kk):
                g = jnp.einsum("tr,tn->rn", act, half_of(grad, 1, kk), preferred_element_type=F32)
                return g.reshape(2, g.shape[0] // 2, g.shape[1])

            return part_of

        d_down = joined(*reduced(cols_of(hidden, cot), 1, 0), 1, core).astype(F32)
        d_gu = joined(*reduced(rows_of(normed_two, pair), 0, 0), 0, core).astype(F32)
        d_out = joined(*reduced(rows_of(mixed, gres_low), 0, 0), 0, core).astype(F32)
        d_q = joined(*reduced(rows_of(normed, cat), 0, 0), 0, core).astype(F32)
        halves = []
        for h in range(2):
            flat = [half_of(g, a, h).reshape(-1) for g, a in zip(small_grads, small_axes)]
            halves.append(jnp.concatenate(flat))
        s = jnp.stack(halves)
        n = s.shape[1]
        s = jnp.pad(s, ((0, 0), (0, -n % 1024))).reshape(2, -1, 128)
        s = s + over_core(s)
        s = lax.dynamic_index_in_dim(s, i, 0, False) + over_x(lax.dynamic_index_in_dim(s, 1 - i, 0, False))
        s = s + over_y(s)
        s = s + over_z(s, 1)
        s = s + over_z(s, 2)
        s = s.reshape(-1)
        done, at = [], 0
        for g, a in zip(small_grads, small_axes):
            shape = tuple(d // 2 if n == a else d for n, d in enumerate(g.shape))
            count = g.size // 2
            done.append(s[at : at + count].reshape(shape))
            at += count
        d_gains, d_up, d_bias, d_group = done
    else:
        def total(g, axis):
            g = lax.psum_scatter(g.astype(BF16), "fsdp", scatter_dimension=axis, tiled=True)
            return lax.psum(g, ("rep", "seq")).astype(F32)

        d_down = total(dot_tn(hidden, cot), 0)
        d_gu = total(dot_tn(normed_two, pair), 0)
        d_out = total(dot_tn(mixed, gres_low), 0)
        d_q = total(dot_tn(normed, cat), 0)
        d_gains, d_up, d_bias, d_group = [total(g, a) for g, a in zip(small_grads, small_axes)]
    d_qk, d_vg, d_low = split_q(d_q)
    d_gu = jnp.stack([d_gu[:, :ff], d_gu[:, ff:]])
    gradients = (d_gains, d_qk, d_vg, d_low, d_up, d_bias, d_group, d_out, d_gu, d_down)
    updated = [adamw_update(*four) for four in zip(masters, gradients, firsts, seconds)]
    return (
        (output[None], grad_tokens[None])
        + gradients
        + tuple(u[0] for u in updated)
        + tuple(u[1] for u in updated)
        + tuple(u[2] for u in updated)
    )


def solution(mesh):
    shape = dict(mesh.shape)
    fast = shape == {"rep": 4, "fsdp": 2, "seq": 4}
    rows = P(("rep", "fsdp"), "seq", None)
    weights = (
        P(None, "fsdp"),
        P(None, "fsdp", None),
        P(None, "fsdp", None),
        P("fsdp", None),
        P(None, "fsdp"),
        P("fsdp"),
        P("fsdp"),
        P("fsdp", None),
        P(None, "fsdp", None),
        P("fsdp", None),
    )
    return jax.shard_map(
        functools.partial(shards, fast),
        mesh=mesh,
        in_specs=(rows, P(("rep", "fsdp"), "seq"), rows) + weights * 3,
        out_specs=(rows, rows) + weights * 4,
        check_vma=False,
    )
```
